32 devices in a mesh: section: 2 (over y), expert: 16 (over z, x, core).
Axes of the slice: x: 2, y: 2, z: 4, core: 2. Of those that a mesh axis runs over, the one named last changes fastest.
Arguments:
- forward_input: bfloat16 [128, 3584], P('expert', 'section'), may hold values from -6 to 6
- forward_route: int32 [128, 8], P('expert'), may hold values from 0 to 15, all different within a row; in each aligned block of 8 rows (0 to 7, 8 to 15, ...) at most 8 rows name the same one
- forward_weight: float32 [128, 8], P('expert'), may hold values from 0.05 to 0.5
- output_grad: bfloat16 [128, 3584], P('expert', 'section'), may hold values from -6 to 6
- backward_route: int32 [128, 8], P('expert'), may hold values from 0 to 15, all different within a row; in each aligned block of 8 rows (0 to 7, 8 to 15, ...) at most 8 rows name the same one
- backward_weight: float32 [128, 8], P('expert'), may hold values from 0.05 to 0.5
- gate_stash: bfloat16 [16, 128, 2560], P('expert', None, 'section'), may hold values from -6 to 6
- up_stash: bfloat16 [16, 128, 2560], P('expert', None, 'section'), may hold values from -6 to 6
- gate_matrix: bfloat16 [16, 2560, 3584], P('expert', 'section'), may hold values from -0.125 to 0.125
- up_matrix: bfloat16 [16, 2560, 3584], P('expert', 'section'), may hold values from -0.125 to 0.125
- down_matrix: bfloat16 [16, 2560, 3584], P('expert', 'section'), may hold values from -0.15625 to 0.15625
Outputs:
- forward_output: bfloat16 [128, 3584], P('expert', 'section')
- input_grad: bfloat16 [128, 3584], P('expert', 'section')
The draws below stay inside these ranges and needn't reach their ends.
Inputs may be any that keep to these rules, and one draw needn't show every extreme that they name: `forward_route`: each row names 8 different experts. In each aligned block of 8 rows (the rows of one index of expert) no expert is named by more than 8 rows, a bound that some block reaches. `backward_route`: as for forward_route.
All inputs are finite; a program needn't handle non-finite values.
Results may differ from the reference program's by a relative error of at most 0.0072.
Values may be sent and summed in bfloat16 or wider, within the bound.
No kernel may reach another device: no remote copies, remote signals or barrier semaphores. Data moves between devices by JAX's collectives and lax.ppermute only.
A program may use at most 128 MiB of HBM per device.

```python
import math
import jax
import jax.numpy as jnp
import numpy as np
from jax import lax

D = 3584
HID = 2560
TOK_DEV = 8
TOPK = 8
EXPERTS = 16
CAP = 8
SLOTS = 128
TOKENS = 128
N_SECTION = 2
N_EXPERT = 16


def spiked(entries, rng, source, target, shards_of, factor):
    owner, partner = [(jnp.arange(entries.shape[dim]) // (entries.shape[dim] // shards_of)).reshape([-1 if axis == dim else 1 for axis in range(entries.ndim)]) for dim in (source, target)]
    chosen = jax.random.permutation(rng, shards_of)[partner]
    strong = (owner == chosen) | (owner == (partner + shards_of // 2) % shards_of)
    return jnp.where(strong, factor * entries, entries)


def shard_levels(key, dims, pieces, smallest, high):
    def one(axis_at, blocks):
        draws = jax.random.uniform(jax.random.fold_in(jax.random.fold_in(key, 6), axis_at), (blocks,), jnp.float32, smallest / len(pieces), high / len(pieces))
        return jnp.repeat(jnp.exp(draws), dims[axis_at] // blocks).reshape((-1,) + (1,) * (len(dims) - axis_at - 1))

    factor_of = one(*pieces[0])
    for cut in pieces[1:]:
        factor_of = factor_of * one(*cut)
    return factor_of


def deal_out(key, own, number, rows, amount, top, bound, skew):
    sequence = jax.random.permutation(key, amount)
    heavy_load, usual = portions_of(amount, rows * top, bound, skew, True), portions_of(amount, rows * top, bound, skew, False)
    places = jnp.arange(amount)

    def named(sizes, offset_by):
        used = int((sizes > 0).sum())
        fixed = max(1, used // 4)
        moved = fixed + (places - fixed + offset_by * (used - fixed)) % max(1, amount - fixed)
        return jnp.zeros((amount,), jnp.int32).at[sequence[jnp.where(places < fixed, places, moved)]].set(jnp.asarray(sizes, jnp.int32))

    sizes = jnp.where(number % 4 == 0, named(heavy_load, number // 4), named(usual, number - number // 4 - 1))
    mixed = jax.random.permutation(jax.random.fold_in(own, 3), amount)
    giver, taker = mixed[0:amount // 2 * 2:2], mixed[1:amount // 2 * 2:2]
    margin = jnp.minimum(sizes[giver] - 1, bound - sizes[taker]) // 2
    margin = jnp.where((giver == sequence[0]) | (taker == sequence[0]) | (sizes[taker] == 0), 0, jnp.maximum(margin, 0))
    moved = jax.random.randint(jax.random.fold_in(own, 4), (amount // 2,), 0, 1 << 20) % (margin + 1)
    sizes = sizes.at[giver].add(-moved).at[taker].add(moved)
    members = jnp.searchsorted(jnp.cumsum(sizes), jnp.arange(rows * top), side="right").astype(jnp.int32)
    table = members.reshape(top, rows).T
    table = table[jax.random.permutation(jax.random.fold_in(own, 1), rows)]
    offset_by = jax.random.randint(jax.random.fold_in(own, 2), (rows, 1), 0, top)
    return jnp.take_along_axis(table, (jnp.arange(top)[None, :] + offset_by) % top, axis=1)


def portions_of(amount, total, reach, skew, full):
    loads = [(1 << 20) // math.isqrt(grade ** skew) + 1 for grade in range(1, amount + 1)]
    largest = reach if full else min(reach, max(-(-total // amount), total * loads[0] // sum(loads)))
    least = 1 if total - largest >= amount - 1 else 0
    holding, rest = [largest] + [least] * (amount - 1), total - largest - least * (amount - 1)
    while rest > 0:
        candidates = [i for i in range(1, amount) if holding[i] < largest] or [i for i in range(1, amount) if holding[i] < reach]
        whole, left = sum([loads[i] for i in candidates]), rest
        for i in candidates:
            addition = min(reach - holding[i], max(1, left * loads[i] // whole), rest)
            holding[i] = holding[i] + addition
            rest = rest - addition
    return np.array(holding)


def gaussian(own_key, extent, deviation, reach, cuts=(), held_as=jnp.bfloat16):
    array = deviation * jax.random.normal(own_key, extent, jnp.float32)
    if cuts:
        array = array * shard_levels(own_key, extent, cuts, -0.22, 0.18)
    return jnp.clip(array, -reach, reach).astype(held_as)


def gaussian_with(stream_key, extent, spread, limit, split, heavy, kind=jnp.bfloat16):
    entries = spread * jax.random.normal(stream_key, extent, jnp.float32)
    if split:
        entries = entries * shard_levels(stream_key, extent, split, -0.22, 0.18)
    return jnp.clip(spiked(entries, jax.random.fold_in(stream_key, 3), *heavy), -limit, limit).astype(kind)


def setup_inputs(seed: int = 0) -> dict:
    key_of = jax.random.split(jax.random.key(seed), 12)
    forward_input = gaussian(key_of[0], (TOKENS, D), 1.0, 6.0, ((0, 16), (1, 2)))
    forward_route_keys = jax.random.split(jax.random.fold_in(key_of[1], 1), TOKENS // TOK_DEV)
    forward_route_turns = jax.random.permutation(jax.random.fold_in(key_of[1], 3), TOKENS // TOK_DEV)
    forward_route = jax.vmap(lambda own, number: deal_out(jax.random.fold_in(key_of[1], 2), own, number, TOK_DEV, EXPERTS, TOPK, CAP, 2))(forward_route_keys, forward_route_turns).reshape((TOKENS, TOPK))
    forward_weight = jnp.clip(jnp.exp(math.log(0.5) - 2.3025851 * jax.random.uniform(key_of[2], (TOKENS, TOPK), jnp.float32) ** shard_levels(key_of[2], (TOKENS, TOPK), ((0, 16),), -0.2, 0.2)), 0.05, 0.5)
    output_grad = gaussian(key_of[3], (TOKENS, D), 1.0, 6.0, ((0, 16), (1, 2)))
    backward_route_keys = jax.random.split(jax.random.fold_in(key_of[4], 1), TOKENS // TOK_DEV)
    backward_route_turns = jax.random.permutation(jax.random.fold_in(key_of[4], 3), TOKENS // TOK_DEV)
    backward_route = jax.vmap(lambda own, number: deal_out(jax.random.fold_in(key_of[4], 2), own, number, TOK_DEV, EXPERTS, TOPK, CAP, 2))(backward_route_keys, backward_route_turns).reshape((TOKENS, TOPK))
    backward_weight = jnp.clip(jnp.exp(math.log(0.5) - 2.3025851 * jax.random.uniform(key_of[5], (TOKENS, TOPK), jnp.float32) ** shard_levels(key_of[5], (TOKENS, TOPK), ((0, 16),), -0.2, 0.2)), 0.05, 0.5)
    gate_stash = gaussian(key_of[6], (EXPERTS, SLOTS, HID), 1.5, 6.0, ((0, 16), (2, 2)))
    up_stash = gaussian(key_of[7], (EXPERTS, SLOTS, HID), 1.0, 6.0, ((0, 16), (2, 2)))
    gate_matrix = gaussian_with(key_of[8], (EXPERTS, HID, D), D ** -0.5, 0.125, ((0, 16), (1, 2)), (1, 2, 2, 2.0))
    up_matrix = gaussian_with(key_of[9], (EXPERTS, HID, D), D ** -0.5, 0.125, ((0, 16), (1, 2)), (1, 2, 2, 2.0))
    down_matrix = gaussian_with(key_of[10], (EXPERTS, HID, D), HID ** -0.5, 0.15625, ((0, 16), (1, 2)), (1, 2, 2, 2.0))
    return dict(forward_input=forward_input, forward_route=forward_route, forward_weight=forward_weight, output_grad=output_grad, backward_route=backward_route, backward_weight=backward_weight, gate_stash=gate_stash, up_stash=up_stash, gate_matrix=gate_matrix, up_matrix=up_matrix, down_matrix=down_matrix)


def slot_table(routes):
    blocked = routes.reshape(N_EXPERT, TOK_DEV, TOPK)
    chosen = (blocked[:, :, :, None] == jnp.arange(EXPERTS, dtype=jnp.int32)[None, None, None, :]).astype(jnp.int32)
    per_token = jnp.sum(chosen, axis=2, dtype=jnp.int32)
    earlier = jnp.cumsum(per_token, axis=1, dtype=jnp.int32) - per_token
    position = jnp.sum(chosen * earlier[:, :, None, :], axis=3, dtype=jnp.int32)
    source = jnp.arange(N_EXPERT, dtype=jnp.int32)[:, None, None] * CAP
    return (source + position).reshape(TOKENS, TOPK).astype(jnp.int32)


def scatter_rows(values, routes, slot_index):
    flattened = values.reshape(TOKENS * TOPK, D)
    buffer = jnp.zeros((EXPERTS, SLOTS, D), values.dtype)
    return buffer.at[routes.reshape(-1), slot_index.reshape(-1)].set(flattened)


def block_parts(factor_rows, factor_cols):
    block_width = HID // N_SECTION
    return jnp.einsum('rsh,shd->srd',
                      factor_rows.reshape(SLOTS, N_SECTION, block_width).astype(jnp.float32),
                      factor_cols.reshape(N_SECTION, block_width, D).astype(jnp.float32),
                      precision=lax.Precision.HIGHEST)


def section_sum(partials):
    rounded = lax.optimization_barrier(partials.astype(jnp.bfloat16))
    return jnp.sum(rounded.astype(jnp.float32), axis=0).astype(jnp.bfloat16)


def expert_forward(operands):
    dispatched, gate_weights, up_weights, down_weights = operands
    gate_value = jnp.dot(dispatched, gate_weights.T, preferred_element_type=jnp.float32)
    up_value = jnp.dot(dispatched, up_weights.T, preferred_element_type=jnp.float32)
    hidden = (jax.nn.silu(gate_value) * up_value).astype(jnp.bfloat16)
    return section_sum(block_parts(hidden, down_weights))


def expert_backward(operands):
    dispatched, gate_saved, up_saved, gate_weights, up_weights, down_weights = operands
    grad_hidden = jnp.dot(dispatched, down_weights.T, preferred_element_type=jnp.float32)
    gate_value = gate_saved.astype(jnp.float32)
    up_value = up_saved.astype(jnp.float32)
    sigmoid_gate = jax.nn.sigmoid(gate_value)
    grad_gate = (grad_hidden * up_value * sigmoid_gate * (1.0 + gate_value * (1.0 - sigmoid_gate))).astype(jnp.bfloat16)
    grad_up = (grad_hidden * gate_value * sigmoid_gate).astype(jnp.bfloat16)
    return section_sum(block_parts(grad_gate, gate_weights) + block_parts(grad_up, up_weights))


def reference(forward_input, forward_route, forward_weight, output_grad, backward_route, backward_weight, gate_stash, up_stash, gate_matrix, up_matrix, down_matrix):
    forward_slot = slot_table(forward_route)
    spread_input = jnp.broadcast_to(forward_input[:, None, :], (TOKENS, TOPK, D))
    forward_dispatch = scatter_rows(spread_input, forward_route, forward_slot)
    expert_output = lax.map(expert_forward, (forward_dispatch, gate_matrix, up_matrix, down_matrix))
    picked = expert_output[forward_route, forward_slot].astype(jnp.float32)
    forward_output = jnp.sum(forward_weight[:, :, None] * picked, axis=1).astype(jnp.bfloat16)
    backward_slot = slot_table(backward_route)
    scaled = (backward_weight[:, :, None] * output_grad[:, None, :].astype(jnp.float32)).astype(jnp.bfloat16)
    grad_dispatch = scatter_rows(scaled, backward_route, backward_slot)
    expert_grad = lax.map(expert_backward, (grad_dispatch, gate_stash, up_stash, gate_matrix, up_matrix, down_matrix))
    input_grad = jnp.sum(expert_grad[backward_route, backward_slot].astype(jnp.float32), axis=1).astype(jnp.bfloat16)
    return forward_output, input_grad
```

```python
import functools

import jax
import jax.numpy as jnp
from jax import lax
from jax.experimental import pallas as pl
from jax.experimental.pallas import tpu as pltpu
from jax.sharding import PartitionSpec as P

LANES = 128
AXES = ("section", "expert")
VMEM = pltpu.MemorySpace.VMEM


def last_last(a, b):
    return lax.dot_general(a, b, (((1,), (1,)), ((), ())), preferred_element_type=jnp.float32)


def last_first(a, b):
    return lax.dot_general(a, b, (((1,), (0,)), ((), ())), preferred_element_type=jnp.float32)


def pack_kernel(expert_count, xf, rf, wf, xb, rb, wb, of, ob):
    tokens, topk = rf.shape
    cols = xf.shape[1]
    lane = lax.broadcasted_iota(jnp.int32, (tokens, LANES), 1)
    row = lax.broadcasted_iota(jnp.int32, (tokens, LANES), 0)
    expert, field = lane % expert_count, lane // expert_count
    for x, r, w, o in ((xf, rf, wf, of), (xb, rb, wb, ob)):
        weight = jnp.zeros((tokens, LANES), jnp.float32)
        named = jnp.zeros((tokens, LANES), jnp.float32)
        for k in range(topk):
            hit = expert == r[:, k : k + 1]
            weight = jnp.where(hit, w[:, k : k + 1], weight)
            named = jnp.where(hit, 1.0, named)
        earlier = jnp.zeros((tokens, LANES), jnp.float32)
        for t in range(tokens - 1):
            earlier = earlier + jnp.where(row > t, named[t : t + 1, :], 0.0)
        high = weight.astype(jnp.bfloat16).astype(jnp.float32)
        low = weight - high
        extra = jnp.where(field == 0, high, jnp.where(field == 1, low, jnp.where(field == 2, earlier, 0.0)))
        o[:, :cols] = x[...]
        o[:, cols:] = extra.astype(jnp.bfloat16)


def pack(expert_count, xf, rf, wf, xb, rb, wb):
    shape = jax.ShapeDtypeStruct((xf.shape[0], xf.shape[1] + LANES), jnp.bfloat16)
    return pl.pallas_call(
        functools.partial(pack_kernel, expert_count), out_shape=(shape, shape), name="pack"
    )(xf, rf, wf, xb, rb, wb)


def chunks(total, size):
    return [(at, min(size, total - at)) for at in range(0, total, size)]


def section_start(j, width, sections):
    if sections == 1:
        return 0
    return pl.multiple_of((lax.axis_index("section") ^ j) * width, LANES)


def field_of(meta, index):
    lane = lax.broadcasted_iota(jnp.int32, meta.shape, 1)
    return jnp.sum(jnp.where(lane == index, meta, 0.0), axis=1, keepdims=True)


def load_rows(groups, sections, width, pieces, rows, held):
    at, metas = 0, []
    for g in range(groups):
        count = pieces[g * sections].shape[0]
        for j in range(sections):
            start = section_start(j, width, sections)
            held[at : at + count, pl.ds(start, width)] = pieces[g * sections + j][:, :width]
        metas.append(pieces[g * sections][:, width:].astype(jnp.float32))
        at += count
    return metas[0] if groups == 1 else jnp.concatenate(metas, axis=0)


def store_rows(groups, sections, width, outs, product):
    for j in range(sections):
        start = section_start(j, width, sections)
        for at, size in chunks(width, 256):
            y = product(start + at, size).astype(jnp.bfloat16)
            row = 0
            for g in range(groups):
                out = outs[g * sections + j]
                out[:, at : at + size] = y[row : row + out.shape[0], :]
                row += out.shape[0]


def forward_kernel(groups, sections, width, experts, *refs):
    n = groups * sections
    pieces, (gate, up, down), outs, (held, hidden) = refs[:n], refs[n : n + 3], refs[n + 3 : 2 * n + 3], refs[2 * n + 3 :]
    meta = load_rows(groups, sections, width, pieces, None, held)
    me = lax.axis_index("expert")
    weight = field_of(meta, me) + field_of(meta, me + experts)
    for at, size in chunks(hidden.shape[1], 256):
        g = last_last(held[...], gate[at : at + size, :])
        u = last_last(held[...], up[at : at + size, :])
        hidden[:, at : at + size] = (g / (1.0 + jnp.exp(-g)) * u).astype(jnp.bfloat16)
    store_rows(
        groups, sections, width, outs,
        lambda start, size: last_first(hidden[...], down[:, pl.ds(start, size)]) * weight,
    )


def backward_kernel(groups, sections, width, experts, capacity, *refs):
    n = groups * sections
    pieces, (block, gate_saved, up_saved, gate, up, down) = refs[:n], refs[n : n + 6]
    outs, (held, grad_gate, grad_up) = refs[n + 6 : 2 * n + 6], refs[2 * n + 6 :]
    meta = load_rows(groups, sections, width, pieces, None, held)
    me = lax.axis_index("expert")
    weight = field_of(meta, me) + field_of(meta, me + experts)
    slot = block[...] * capacity + field_of(meta, me + 2 * experts).astype(jnp.int32)
    slot = jnp.where(weight > 0.0, slot, -1)
    place = lax.broadcasted_iota(jnp.int32, (held.shape[0], gate_saved.shape[0]), 1)
    pick = jnp.where(place == slot, 1.0, 0.0).astype(jnp.bfloat16)
    for at, size in chunks(grad_gate.shape[1], 256):
        part = slice(at, at + size)
        grad = last_last(held[...], down[part, :]) * weight
        g = last_first(pick, gate_saved[:, part])
        u = last_first(pick, up_saved[:, part])
        q = 1.0 / (1.0 + jnp.exp(-g))
        grad_gate[:, part] = (grad * u * q * (1.0 + g * (1.0 - q))).astype(jnp.bfloat16)
        grad_up[:, part] = (grad * g * q).astype(jnp.bfloat16)
    store_rows(
        groups, sections, width, outs,
        lambda start, size: last_first(grad_gate[...], gate[:, pl.ds(start, size)])
        + last_first(grad_up[...], up[:, pl.ds(start, size)]),
    )


def expert_call(kernel, name, pieces, sections, width, extra, weights, scratch):
    outs = tuple(jax.ShapeDtypeStruct((p.shape[0], width), jnp.bfloat16) for p in pieces)
    weights = [pltpu.with_memory_space_constraint(w, VMEM) for w in weights]
    return pl.pallas_call(
        kernel,
        out_shape=outs,
        scratch_shapes=scratch,
        compiler_params=pltpu.CompilerParams(vmem_limit_bytes=24 << 20),
        name=name,
    )(*pieces, *extra, *weights)


def experts_forward(pieces, sections, width, experts, weights):
    rows = sum(p.shape[0] for p in pieces) // sections
    units, features = weights[0].shape
    return expert_call(
        functools.partial(forward_kernel, len(pieces) // sections, sections, width, experts),
        "experts_forward", pieces, sections, width, [], weights,
        [pltpu.VMEM((rows, features), jnp.bfloat16), pltpu.VMEM((rows, units), jnp.bfloat16)],
    )


def experts_backward(pieces, sections, width, experts, capacity, block, stash, weights):
    rows = sum(p.shape[0] for p in pieces) // sections
    units, features = weights[0].shape
    return expert_call(
        functools.partial(backward_kernel, len(pieces) // sections, sections, width, experts, capacity),
        "experts_backward", pieces, sections, width, [block, *stash], weights,
        [pltpu.VMEM((rows, features), jnp.bfloat16)] + [pltpu.VMEM((rows, units), jnp.bfloat16)] * 2,
    )


def move(value, mask, devices):
    return lax.ppermute(value, AXES, [(i, i ^ mask) for i in range(devices)])


Z = (8, 4, 12)
X, Y, CORE = 2, 16, 1


def spread(message):
    tokens, cols = message.shape
    held = message[None]
    for mask in Z[:2]:
        held = jnp.concatenate([held, move(held, mask, 32)], axis=0)
    held = held.reshape(4 * tokens, cols)
    own = [held, move(held, Y, 32), move(held, X, 32), move(held, X ^ Y, 32)]
    return own + [move(p, CORE, 32) for p in own]


def collect(pieces, tokens):
    other = [move(p, CORE, 32) for p in pieces[4:]]
    own = [
        (a.astype(jnp.float32) + b.astype(jnp.float32)).astype(jnp.bfloat16) for a, b in zip(pieces[:4], other)
    ]
    parts = [own[0], move(own[1], Y, 32), move(own[2], X, 32), move(own[3], X ^ Y, 32)]
    total = sum(p.astype(jnp.float32) for p in parts).astype(jnp.bfloat16)
    rows = [total[k * tokens : (k + 1) * tokens] for k in range(4)]
    parts = [rows[0]] + [move(rows[k + 1], Z[k], 32) for k in range(3)]
    return sum(p.astype(jnp.float32) for p in parts).astype(jnp.bfloat16)


def spread_any(message, width):
    held = lax.all_gather(message, "expert", axis=0, tiled=True)
    whole = lax.all_gather(held[:, :width], "section", axis=1, tiled=True)
    return [jnp.concatenate([whole, held[:, width:]], axis=1)]


def collect_any(pieces):
    summed = lax.psum_scatter(pieces[0], "section", scatter_dimension=1, tiled=True)
    return lax.psum_scatter(summed, "expert", scatter_dimension=0, tiled=True)


def shards(
    forward_input, forward_route, forward_weight, output_grad, backward_route, backward_weight,
    gate_stash, up_stash, gate_matrix, up_matrix, down_matrix,
):
    expert_count, section_count = lax.axis_size("expert"), lax.axis_size("section")
    tokens, width = forward_input.shape
    capacity = gate_stash.shape[1] // expert_count
    weights = (gate_matrix[0], up_matrix[0], down_matrix[0])
    stash = (gate_stash[0], up_stash[0])
    message_f, message_b = pack(
        expert_count, forward_input, forward_route, forward_weight, output_grad, backward_route, backward_weight
    )
    if (section_count, expert_count) == (2, 16):
        sections = 2
        mask = jnp.array([c ^ x ^ z for c in (0, CORE) for x in (0, X) for z in (0, 8, 4, 12)], jnp.int32)
        order = lax.axis_index("expert") ^ mask
        pieces_f, pieces_b = spread(message_f), spread(message_b)
        gather = functools.partial(collect, tokens=tokens)
    else:
        sections = 1
        order = jnp.arange(expert_count, dtype=jnp.int32)
        pieces_f, pieces_b = spread_any(message_f, width), spread_any(message_b, width)
        width, gather = width * section_count, collect_any
    block = jnp.repeat(order, tokens)[:, None]
    done_f = experts_forward(pieces_f, sections, width, expert_count, weights)
    done_b = experts_backward(pieces_b, sections, width, expert_count, capacity, block, stash, weights)
    return gather(list(done_f)), gather(list(done_b))


def solution(mesh):
    split, rows, stash, matrix = (
        P("expert", "section"), P("expert", None), P("expert", None, "section"), P("expert", "section", None)
    )
    in_specs = (split, rows, rows, split, rows, rows, stash, stash, matrix, matrix, matrix)
    return jax.shard_map(shards, mesh=mesh, in_specs=in_specs, out_specs=(split, split), check_vma=False)
```

```python
import functools

import jax
import jax.numpy as jnp
from jax import lax
from jax.experimental import pallas as pl
from jax.experimental.pallas import tpu as pltpu
from jax.sharding import PartitionSpec as P

LANES = 128
AXES = ("section", "expert")
VMEM = pltpu.MemorySpace.VMEM


def last_last(a, b):
    return lax.dot_general(a, b, (((1,), (1,)), ((), ())), preferred_element_type=jnp.float32)


def last_first(a, b):
    return lax.dot_general(a, b, (((1,), (0,)), ((), ())), preferred_element_type=jnp.float32)


def pack_kernel(expert_count, *refs):
    given, (of, ob), held, arrived = refs[:6], refs[6:8], refs[8:14], refs[14]
    copies = [pltpu.make_async_copy(a, b, arrived.at[i]) for i, (a, b) in enumerate(zip(given, held))]
    for copy in copies:
        copy.start()
    for copy in copies:
        copy.wait()
    xf, rf, wf, xb, rb, wb = held
    tokens, topk = rf.shape
    cols = xf.shape[1]
    lane = lax.broadcasted_iota(jnp.int32, (tokens, LANES), 1)
    row = lax.broadcasted_iota(jnp.int32, (tokens, LANES), 0)
    expert, field = lane % expert_count, lane // expert_count
    for x, r, w, o in ((xf, rf, wf, of), (xb, rb, wb, ob)):
        weight = jnp.zeros((tokens, LANES), jnp.float32)
        named = jnp.zeros((tokens, LANES), jnp.float32)
        for k in range(topk):
            hit = expert == r[:, k : k + 1]
            weight = jnp.where(hit, w[:, k : k + 1], weight)
            named = jnp.where(hit, 1.0, named)
        earlier = jnp.zeros((tokens, LANES), jnp.float32)
        for t in range(tokens - 1):
            earlier = earlier + jnp.where(row > t, named[t : t + 1, :], 0.0)
        high = weight.astype(jnp.bfloat16).astype(jnp.float32)
        low = weight - high
        extra = jnp.where(field == 0, high, jnp.where(field == 1, low, jnp.where(field == 2, earlier, 0.0)))
        o[:, :cols] = x[...]
        o[:, cols:] = extra.astype(jnp.bfloat16)


def pack(expert_count, *given):
    tokens, cols = given[0].shape
    shape = jax.ShapeDtypeStruct((tokens, cols + LANES), jnp.bfloat16)
    given = [pltpu.with_memory_space_constraint(a, pltpu.MemorySpace.HBM) for a in given]
    return pl.pallas_call(
        functools.partial(pack_kernel, expert_count),
        out_shape=(shape, shape),
        in_specs=[pl.BlockSpec(memory_space=pltpu.MemorySpace.HBM)] * 6,
        scratch_shapes=[pltpu.VMEM(a.shape, a.dtype) for a in given] + [pltpu.SemaphoreType.DMA((6,))],
        compiler_params=pltpu.CompilerParams(vmem_limit_bytes=2 << 20),
        cost_estimate=pl.CostEstimate(flops=40_000_000_000, bytes_accessed=100_000_000, transcendentals=0),
        name="pack",
    )(*given)


def chunks(total, size):
    return [(at, min(size, total - at)) for at in range(0, total, size)]


def section_start(j, width, sections):
    if sections == 1:
        return 0
    return pl.multiple_of((lax.axis_index("section") ^ j) * width, LANES)


def field_of(meta, index):
    lane = lax.broadcasted_iota(jnp.int32, meta.shape, 1)
    return jnp.sum(jnp.where(lane == index, meta, 0.0), axis=1, keepdims=True)


def load_rows(groups, sections, width, pieces, held):
    at, metas = 0, []
    for g in range(groups):
        count = pieces[g * sections].shape[0]
        for j in range(sections):
            start = section_start(j, width, sections)
            held[at : at + count, pl.ds(start, width)] = pieces[g * sections + j][:, :width]
        metas.append(pieces[g * sections][:, width:].astype(jnp.float32))
        at += count
    return metas[0] if groups == 1 else jnp.concatenate(metas, axis=0)


def store_rows(groups, sections, width, outs, product):
    for j in range(sections):
        start = section_start(j, width, sections)
        for at, size in chunks(width, 256):
            y = product(start + at, size).astype(jnp.bfloat16)
            row = 0
            for g in range(groups):
                out = outs[g * sections + j]
                out[:, at : at + size] = y[row : row + out.shape[0], :]
                row += out.shape[0]


def hidden_kernel(groups, sections, width, experts, *refs):
    n = groups * sections
    pieces, (gate, up), (hidden, scale), (held,) = refs[:n], refs[n : n + 2], refs[n + 2 : n + 4], refs[n + 4 :]
    meta = load_rows(groups, sections, width, pieces, held)
    me = lax.axis_index("expert")
    scale[...] = field_of(meta, me) + field_of(meta, me + experts)
    for at, size in chunks(hidden.shape[1], 256):
        g = last_last(held[...], gate[at : at + size, :])
        u = last_last(held[...], up[at : at + size, :])
        hidden[:, at : at + size] = (g / (1.0 + jnp.exp(-g)) * u).astype(jnp.bfloat16)


def down_kernel(groups, sections, width, hidden, scale, down, *outs):
    store_rows(
        groups, sections, width, outs,
        lambda start, size: last_first(hidden[...], down[:, pl.ds(start, size)]) * scale[...],
    )


def sender_of_rows(rows, tokens, order, me):
    place = lax.broadcasted_iota(jnp.int32, (rows, 1), 0) // tokens
    block = jnp.zeros((rows, 1), jnp.int32) if order is None else jnp.full((rows, 1), me)
    for bit in range((rows // tokens - 1).bit_length()):
        block = block ^ (place >> bit & 1) * (1 << bit if order is None else order[1 << bit])
    return block


def backward_kernel(groups, sections, width, experts, capacity, tokens, order, *refs):
    n = groups * sections
    pieces, (gate_saved, up_saved, gate, up, down) = refs[:n], refs[n : n + 5]
    outs, (held, grad_gate, grad_up) = refs[n + 5 : 2 * n + 5], refs[2 * n + 5 :]
    meta = load_rows(groups, sections, width, pieces, held)
    me = lax.axis_index("expert")
    weight = field_of(meta, me) + field_of(meta, me + experts)
    block = sender_of_rows(held.shape[0], tokens, order, me)
    slot = block * capacity + field_of(meta, me + 2 * experts).astype(jnp.int32)
    slot = jnp.where(weight > 0.0, slot, -1)
    place = lax.broadcasted_iota(jnp.int32, (held.shape[0], gate_saved.shape[0]), 1)
    pick = jnp.where(place == slot, 1.0, 0.0).astype(jnp.bfloat16)
    for at, size in chunks(grad_gate.shape[1], 256):
        part = slice(at, at + size)
        grad = last_last(held[...], down[part, :]) * weight
        g = last_first(pick, gate_saved[:, part])
        u = last_first(pick, up_saved[:, part])
        q = 1.0 / (1.0 + jnp.exp(-g))
        grad_gate[:, part] = (grad * u * q * (1.0 + g * (1.0 - q))).astype(jnp.bfloat16)
        grad_up[:, part] = (grad * g * q).astype(jnp.bfloat16)
    store_rows(
        groups, sections, width, outs,
        lambda start, size: last_first(grad_gate[...], gate[:, pl.ds(start, size)])
        + last_first(grad_up[...], up[:, pl.ds(start, size)]),
    )


def expert_call(kernel, name, shapes, weights, given, scratch=()):
    rows = given[0].shape[0]
    weights = [pltpu.with_memory_space_constraint(w, VMEM) for w in weights]
    cost = pl.CostEstimate(
        flops=sum(256 * w.size for w in weights), bytes_accessed=sum(2 * w.size for w in weights), transcendentals=0
    )
    return pl.pallas_call(
        kernel,
        out_shape=shapes,
        scratch_shapes=scratch,
        compiler_params=pltpu.CompilerParams(vmem_limit_bytes=24 << 20),
        cost_estimate=cost,
        name=name,
    )(*given, *weights)


def like_pieces(pieces, width):
    return tuple(jax.ShapeDtypeStruct((p.shape[0], width), jnp.bfloat16) for p in pieces)


def rows_of(pieces, sections):
    return sum(p.shape[0] for p in pieces) // sections


def forward_hidden(pieces, sections, width, experts, weights):
    rows, (units, features) = rows_of(pieces, sections), weights[0].shape
    return expert_call(
        functools.partial(hidden_kernel, len(pieces) // sections, sections, width, experts),
        "forward_hidden",
        (jax.ShapeDtypeStruct((rows, units), jnp.bfloat16), jax.ShapeDtypeStruct((rows, 1), jnp.float32)),
        weights, pieces, [pltpu.VMEM((rows, features), jnp.bfloat16)],
    )


def forward_down(pieces, sections, width, hidden, scale, weight):
    return expert_call(
        functools.partial(down_kernel, len(pieces) // sections, sections, width),
        "forward_down", like_pieces(pieces, width), [weight], [hidden, scale],
    )


def experts_backward(pieces, sections, width, experts, capacity, tokens, order, stash, weights):
    rows, (units, features) = rows_of(pieces, sections), weights[0].shape
    return expert_call(
        functools.partial(
            backward_kernel, len(pieces) // sections, sections, width, experts, capacity, tokens, order
        ),
        "experts_backward", like_pieces(pieces, width), weights, [*pieces, *stash],
        [pltpu.VMEM((rows, features), jnp.bfloat16)] + [pltpu.VMEM((rows, units), jnp.bfloat16)] * 2,
    )


def move(value, mask, devices):
    return lax.ppermute(value, AXES, [(i, i ^ mask) for i in range(devices)])


Z = (8, 4, 12)
X, Y, CORE = 2, 16, 1


def after(value, *others):
    return lax.optimization_barrier((value, *others))[0]


def spread_line(message):
    tokens, cols = message.shape
    held = message[None]
    for mask in Z[:2]:
        held = jnp.concatenate([held, move(held, mask, 32)], axis=0)
    return held.reshape(4 * tokens, cols)


def spread_plane(held):
    return [held, move(held, Y, 32), move(held, X, 32), move(held, X ^ Y, 32)]


def swap(pieces):
    return [move(p, CORE, 32) for p in pieces]


def add(*parts):
    return sum(p.astype(jnp.float32) for p in parts).astype(jnp.bfloat16)


def collect_plane(own):
    return add(own[0], move(own[1], Y, 32), move(own[2], X, 32), move(own[3], X ^ Y, 32))


def collect_line(total, tokens):
    rows = [total[k * tokens : (k + 1) * tokens] for k in range(4)]
    return add(rows[0], *[move(rows[k + 1], Z[k], 32) for k in range(3)])


def spread_any(message, width):
    held = lax.all_gather(message, "expert", axis=0, tiled=True)
    whole = lax.all_gather(held[:, :width], "section", axis=1, tiled=True)
    return [jnp.concatenate([whole, held[:, width:]], axis=1)]


def collect_any(pieces):
    summed = lax.psum_scatter(pieces[0], "section", scatter_dimension=1, tiled=True)
    return lax.psum_scatter(summed, "expert", scatter_dimension=0, tiled=True)


def shards(
    forward_input, forward_route, forward_weight, output_grad, backward_route, backward_weight,
    gate_stash, up_stash, gate_matrix, up_matrix, down_matrix,
):
    expert_count, section_count = lax.axis_size("expert"), lax.axis_size("section")
    tokens, width = forward_input.shape
    capacity = gate_stash.shape[1] // expert_count
    weights = (gate_matrix[0], up_matrix[0], down_matrix[0])
    stash = (gate_stash[0], up_stash[0])
    message_f, message_b = pack(
        expert_count, forward_input, forward_route, forward_weight, output_grad, backward_route, backward_weight
    )
    if (section_count, expert_count) != (2, 16):
        whole = width * section_count
        pieces_f, pieces_b = spread_any(message_f, width), spread_any(message_b, width)
        hidden, scale = forward_hidden(pieces_f, 1, whole, expert_count, weights[:2])
        done_f = forward_down(pieces_f, 1, whole, hidden, scale, weights[2])
        done_b = experts_backward(pieces_b, 1, whole, expert_count, capacity, tokens, None, stash, weights)
        return collect_any(done_f), collect_any(done_b)
    order = [c ^ x ^ z for c in (0, CORE) for x in (0, X) for z in (0, *Z)]
    line_b, line_f = spread_line(message_b), spread_line(message_f)
    plane_b = spread_plane(line_b)
    plane_f = spread_plane(line_f)
    pieces_b = plane_b + swap(plane_b)
    done_b = experts_backward(pieces_b, 2, width, expert_count, capacity, tokens, order, stash, weights)
    plane_f = [line_f] + [after(p, done_b[0]) for p in plane_f[1:]]
    pieces_f = plane_f + swap(plane_f)
    hidden, scale = forward_hidden(pieces_f, 2, width, expert_count, weights[:2])
    own_b = [add(a, b) for a, b in zip(done_b[:4], swap(done_b[4:]))]
    done_f0 = None
    done_f = forward_down(pieces_f, 2, width, hidden, scale, weights[2])
    own_f = [add(a, b) for a, b in zip(done_f[:4], swap(done_f[4:]))]
    return collect_line(collect_plane(own_f), tokens), collect_line(collect_plane(own_b), tokens)


def solution(mesh):
    split, rows, stash, matrix = (
        P("expert", "section"), P("expert", None), P("expert", None, "section"), P("expert", "section", None)
    )
    in_specs = (split, rows, rows, split, rows, rows, stash, stash, matrix, matrix, matrix)
    return jax.shard_map(shards, mesh=mesh, in_specs=in_specs, out_specs=(split, split), check_vma=False)
```

```python
import functools

import jax
import jax.numpy as jnp
from jax import lax
from jax.experimental import pallas as pl
from jax.experimental.pallas import tpu as pltpu
from jax.sharding import PartitionSpec as P

LANES = 128
AXES = ("section", "expert")
VMEM = pltpu.MemorySpace.VMEM


def last_last(a, b):
    return lax.dot_general(a, b, (((1,), (1,)), ((), ())), preferred_element_type=jnp.float32)


def last_first(a, b):
    return lax.dot_general(a, b, (((1,), (0,)), ((), ())), preferred_element_type=jnp.float32)


def pack_kernel(expert_count, *refs):
    given, (of, ob), held, arrived = refs[:6], refs[6:8], refs[8:14], refs[14]
    copies = [pltpu.make_async_copy(a, b, arrived.at[i]) for i, (a, b) in enumerate(zip(given, held))]
    for copy in copies:
        copy.start()
    for copy in copies:
        copy.wait()
    xf, rf, wf, xb, rb, wb = held
    tokens, topk = rf.shape
    cols = xf.shape[1]
    lane = lax.broadcasted_iota(jnp.int32, (tokens, LANES), 1)
    row = lax.broadcasted_iota(jnp.int32, (tokens, LANES), 0)
    expert, field = lane % expert_count, lane // expert_count
    for x, r, w, o in ((xf, rf, wf, of), (xb, rb, wb, ob)):
        weight = jnp.zeros((tokens, LANES), jnp.float32)
        named = jnp.zeros((tokens, LANES), jnp.float32)
        for k in range(topk):
            hit = expert == r[:, k : k + 1]
            weight = jnp.where(hit, w[:, k : k + 1], weight)
            named = jnp.where(hit, 1.0, named)
        earlier = jnp.zeros((tokens, LANES), jnp.float32)
        for t in range(tokens - 1):
            earlier = earlier + jnp.where(row > t, named[t : t + 1, :], 0.0)
        high = weight.astype(jnp.bfloat16).astype(jnp.float32)
        low = weight - high
        extra = jnp.where(field == 0, high, jnp.where(field == 1, low, jnp.where(field == 2, earlier, 0.0)))
        o[:, :cols] = x[...]
        o[:, cols:] = extra.astype(jnp.bfloat16)


def pack(expert_count, *given):
    tokens, cols = given[0].shape
    shape = jax.ShapeDtypeStruct((tokens, cols + LANES), jnp.bfloat16)
    given = [pltpu.with_memory_space_constraint(a, pltpu.MemorySpace.HBM) for a in given]
    return pl.pallas_call(
        functools.partial(pack_kernel, expert_count),
        out_shape=(shape, shape),
        in_specs=[pl.BlockSpec(memory_space=pltpu.MemorySpace.HBM)] * 6,
        scratch_shapes=[pltpu.VMEM(a.shape, a.dtype) for a in given] + [pltpu.SemaphoreType.DMA((6,))],
        compiler_params=pltpu.CompilerParams(vmem_limit_bytes=2 << 20),
        cost_estimate=pl.CostEstimate(flops=40_000_000_000, bytes_accessed=100_000_000, transcendentals=0),
        name="pack",
    )(*given)


def chunks(total, size):
    return [(at, min(size, total - at)) for at in range(0, total, size)]


def section_start(j, width, sections):
    if sections == 1:
        return 0
    return pl.multiple_of((lax.axis_index("section") ^ j) * width, LANES)


def field_of(meta, index):
    lane = lax.broadcasted_iota(jnp.int32, meta.shape, 1)
    return jnp.sum(jnp.where(lane == index, meta, 0.0), axis=1, keepdims=True)


def load_rows(groups, sections, width, pieces, held):
    at, metas = 0, []
    for g in range(groups):
        count = pieces[g * sections].shape[0]
        for j in range(sections):
            start = section_start(j, width, sections)
            held[at : at + count, pl.ds(start, width)] = pieces[g * sections + j][:, :width]
        metas.append(pieces[g * sections][:, width:].astype(jnp.float32))
        at += count
    return metas[0] if groups == 1 else jnp.concatenate(metas, axis=0)


def store_rows(groups, sections, width, outs, product):
    for j in range(sections):
        start = section_start(j, width, sections)
        for at, size in chunks(width, 256):
            y = product(start + at, size).astype(jnp.bfloat16)
            row = 0
            for g in range(groups):
                out = outs[g * sections + j]
                out[:, at : at + size] = y[row : row + out.shape[0], :]
                row += out.shape[0]


def hidden_kernel(groups, sections, width, experts, *refs):
    n = groups * sections
    pieces, (gate, up), (hidden, scale), (held,) = refs[:n], refs[n : n + 2], refs[n + 2 : n + 4], refs[n + 4 :]
    meta = load_rows(groups, sections, width, pieces, held)
    me = lax.axis_index("expert")
    scale[...] = field_of(meta, me) + field_of(meta, me + experts)
    for at, size in chunks(hidden.shape[1], 128):
        g = last_last(gate[at : at + size, :], held[...])
        u = last_last(up[at : at + size, :], held[...])
        hidden[:, at : at + size] = (g / (1.0 + jnp.exp(-g)) * u).T.astype(jnp.bfloat16)


def down_kernel(groups, sections, width, hidden, scale, down, *outs):
    store_rows(
        groups, sections, width, outs,
        lambda start, size: last_first(hidden[...], down[:, pl.ds(start, size)]) * scale[...],
    )


def sender_of_rows(rows, tokens, order, me):
    place = lax.broadcasted_iota(jnp.int32, (rows, 1), 0) // tokens
    block = jnp.zeros((rows, 1), jnp.int32) if order is None else jnp.full((rows, 1), me)
    for bit in range((rows // tokens - 1).bit_length()):
        block = block ^ (place >> bit & 1) * (1 << bit if order is None else order[1 << bit])
    return block


def backward_kernel(groups, sections, width, experts, capacity, tokens, order, *refs):
    n = groups * sections
    pieces, (gate_saved, up_saved, gate, up, down) = refs[:n], refs[n : n + 5]
    outs, (held, grad_gate, grad_up) = refs[n + 5 : 2 * n + 5], refs[2 * n + 5 :]
    meta = load_rows(groups, sections, width, pieces, held)
    me = lax.axis_index("expert")
    weight = field_of(meta, me) + field_of(meta, me + experts)
    block = sender_of_rows(held.shape[0], tokens, order, me)
    slot = block * capacity + field_of(meta, me + 2 * experts).astype(jnp.int32)
    slot = jnp.where(weight > 0.0, slot, -1)
    place = lax.broadcasted_iota(jnp.int32, (held.shape[0], gate_saved.shape[0]), 1)
    pick = jnp.where(place == slot, 1.0, 0.0).astype(jnp.bfloat16)
    for at, size in chunks(grad_gate.shape[1], 128):
        part = slice(at, at + size)
        grad = last_last(down[part, :], held[...]).T * weight
        g = last_first(pick, gate_saved[:, part])
        u = last_first(pick, up_saved[:, part])
        q = 1.0 / (1.0 + jnp.exp(-g))
        grad_gate[:, part] = (grad * u * q * (1.0 + g * (1.0 - q))).astype(jnp.bfloat16)
        grad_up[:, part] = (grad * g * q).astype(jnp.bfloat16)
    store_rows(
        groups, sections, width, outs,
        lambda start, size: last_first(grad_gate[...], gate[:, pl.ds(start, size)])
        + last_first(grad_up[...], up[:, pl.ds(start, size)]),
    )


def expert_call(kernel, name, shapes, weights, given, scratch=()):
    rows = given[0].shape[0]
    weights = [pltpu.with_memory_space_constraint(w, VMEM) for w in weights]
    cost = pl.CostEstimate(
        flops=sum(256 * w.size for w in weights), bytes_accessed=sum(2 * w.size for w in weights), transcendentals=0
    )
    return pl.pallas_call(
        kernel,
        out_shape=shapes,
        scratch_shapes=scratch,
        compiler_params=pltpu.CompilerParams(vmem_limit_bytes=24 << 20),
        cost_estimate=cost,
        name=name,
    )(*given, *weights)


def like_pieces(pieces, width):
    return tuple(jax.ShapeDtypeStruct((p.shape[0], width), jnp.bfloat16) for p in pieces)


def rows_of(pieces, sections):
    return sum(p.shape[0] for p in pieces) // sections


def forward_hidden(pieces, sections, width, experts, weights):
    rows, (units, features) = rows_of(pieces, sections), weights[0].shape
    return expert_call(
        functools.partial(hidden_kernel, len(pieces) // sections, sections, width, experts),
        "forward_hidden",
        (jax.ShapeDtypeStruct((rows, units), jnp.bfloat16), jax.ShapeDtypeStruct((rows, 1), jnp.float32)),
        weights, pieces, [pltpu.VMEM((rows, features), jnp.bfloat16)],
    )


def forward_down(pieces, sections, width, hidden, scale, weight):
    return expert_call(
        functools.partial(down_kernel, len(pieces) // sections, sections, width),
        "forward_down", like_pieces(pieces, width), [weight], [hidden, scale],
    )


def experts_backward(pieces, sections, width, experts, capacity, tokens, order, stash, weights):
    rows, (units, features) = rows_of(pieces, sections), weights[0].shape
    return expert_call(
        functools.partial(
            backward_kernel, len(pieces) // sections, sections, width, experts, capacity, tokens, order
        ),
        "experts_backward", like_pieces(pieces, width), weights, [*pieces, *stash],
        [pltpu.VMEM((rows, features), jnp.bfloat16)] + [pltpu.VMEM((rows, units), jnp.bfloat16)] * 2,
    )


def move(value, mask, devices):
    return lax.ppermute(value, AXES, [(i, i ^ mask) for i in range(devices)])


Z = (8, 4, 12)
X, Y, CORE = 2, 16, 1


def after(value, *others):
    return lax.optimization_barrier((value, *others))[0]


def spread_line(message):
    tokens, cols = message.shape
    held = message[None]
    for mask in Z[:2]:
        held = jnp.concatenate([held, move(held, mask, 32)], axis=0)
    return held.reshape(4 * tokens, cols)


def spread_shot(message):
    parts = [move(message, mask, 32) for mask in Z[::-1]][::-1]
    return jnp.concatenate([message, *parts], axis=0)


def spread_plane(held):
    return [held, move(held, Y, 32), move(held, X, 32), move(held, X ^ Y, 32)]


def swap(pieces):
    return [move(p, CORE, 32) for p in pieces[::-1]][::-1]


def add(*parts):
    return sum(p.astype(jnp.float32) for p in parts).astype(jnp.bfloat16)


def collect_plane(own):
    return add(own[0], move(own[3], X ^ Y, 32), move(own[1], Y, 32), move(own[2], X, 32))


def collect_line(total, tokens):
    rows = [total[k * tokens : (k + 1) * tokens] for k in range(4)]
    return add(rows[0], *[move(rows[k + 1], Z[k], 32) for k in (2,1,0)])


def spread_any(message, width):
    held = lax.all_gather(message, "expert", axis=0, tiled=True)
    whole = lax.all_gather(held[:, :width], "section", axis=1, tiled=True)
    return [jnp.concatenate([whole, held[:, width:]], axis=1)]


def collect_any(pieces):
    summed = lax.psum_scatter(pieces[0], "section", scatter_dimension=1, tiled=True)
    return lax.psum_scatter(summed, "expert", scatter_dimension=0, tiled=True)


def shards(
    forward_input, forward_route, forward_weight, output_grad, backward_route, backward_weight,
    gate_stash, up_stash, gate_matrix, up_matrix, down_matrix,
):
    expert_count, section_count = lax.axis_size("expert"), lax.axis_size("section")
    tokens, width = forward_input.shape
    capacity = gate_stash.shape[1] // expert_count
    weights = (gate_matrix[0], up_matrix[0], down_matrix[0])
    stash = (gate_stash[0], up_stash[0])
    message_f, message_b = pack(
        expert_count, forward_input, forward_route, forward_weight, output_grad, backward_route, backward_weight
    )
    if (section_count, expert_count) != (2, 16):
        whole = width * section_count
        pieces_f, pieces_b = spread_any(message_f, width), spread_any(message_b, width)
        hidden, scale = forward_hidden(pieces_f, 1, whole, expert_count, weights[:2])
        done_f = forward_down(pieces_f, 1, whole, hidden, scale, weights[2])
        done_b = experts_backward(pieces_b, 1, whole, expert_count, capacity, tokens, None, stash, weights)
        return collect_any(done_f), collect_any(done_b)
    order = [c ^ x ^ z for c in (0, CORE) for x in (0, X) for z in (0, *Z)]
    line_b, line_f = spread_shot(message_b), spread_line(message_f)
    plane_b = spread_plane(line_b)
    plane_f = spread_plane(line_f)
    pieces_b = plane_b + swap(plane_b)
    done_b = experts_backward(pieces_b, 2, width, expert_count, capacity, tokens, order, stash, weights)
    plane_f = [line_f] + [after(p, done_b[0]) for p in plane_f[1:]]
    pieces_f = plane_f + swap(plane_f)
    hidden, scale = forward_hidden(pieces_f, 2, width, expert_count, weights[:2])
    own_b = [add(a, b) for a, b in zip(done_b[:4], swap(done_b[4:]))]
    done_f = forward_down(pieces_f, 2, width, hidden, scale, weights[2])
    own_f = [add(a, b) for a, b in zip(done_f[:4], swap(done_f[4:]))]
    return collect_line(collect_plane(own_f), tokens), collect_line(collect_plane(own_b), tokens)


def solution(mesh):
    split, rows, stash, matrix = (
        P("expert", "section"), P("expert", None), P("expert", None, "section"), P("expert", "section", None)
    )
    in_specs = (split, rows, rows, split, rows, rows, stash, stash, matrix, matrix, matrix)
    return jax.shard_map(shards, mesh=mesh, in_specs=in_specs, out_specs=(split, split), check_vma=False)
```

```python
import functools

import jax
import jax.numpy as jnp
from jax import lax
from jax.experimental import pallas as pl
from jax.experimental.pallas import tpu as pltpu
from jax.sharding import PartitionSpec as P

LANES = 128
AXES = ("section", "expert")
VMEM = pltpu.MemorySpace.VMEM


def last_last(a, b):
    return lax.dot_general(a, b, (((1,), (1,)), ((), ())), preferred_element_type=jnp.float32)


def last_first(a, b):
    return lax.dot_general(a, b, (((1,), (0,)), ((), ())), preferred_element_type=jnp.float32)


def pack_kernel(expert_count, *refs):
    given, (of, ob), held, arrived = refs[:6], refs[6:8], refs[8:14], refs[14]
    copies = [pltpu.make_async_copy(a, b, arrived.at[i]) for i, (a, b) in enumerate(zip(given, held))]
    for copy in copies:
        copy.start()
    for copy in copies:
        copy.wait()
    xf, rf, wf, xb, rb, wb = held
    tokens, topk = rf.shape
    cols = xf.shape[1]
    lane = lax.broadcasted_iota(jnp.int32, (tokens, LANES), 1)
    row = lax.broadcasted_iota(jnp.int32, (tokens, LANES), 0)
    expert, field = lane % expert_count, lane // expert_count
    for x, r, w, o in ((xf, rf, wf, of), (xb, rb, wb, ob)):
        weight = jnp.zeros((tokens, LANES), jnp.float32)
        named = jnp.zeros((tokens, LANES), jnp.float32)
        for k in range(topk):
            hit = expert == r[:, k : k + 1]
            weight = jnp.where(hit, w[:, k : k + 1], weight)
            named = jnp.where(hit, 1.0, named)
        earlier = jnp.zeros((tokens, LANES), jnp.float32)
        for t in range(tokens - 1):
            earlier = earlier + jnp.where(row > t, named[t : t + 1, :], 0.0)
        high = weight.astype(jnp.bfloat16).astype(jnp.float32)
        low = weight - high
        extra = jnp.where(field == 0, high, jnp.where(field == 1, low, jnp.where(field == 2, earlier, 0.0)))
        o[:, :cols] = x[...]
        o[:, cols:] = extra.astype(jnp.bfloat16)


def pack(expert_count, *given):
    tokens, cols = given[0].shape
    shape = jax.ShapeDtypeStruct((tokens, cols + LANES), jnp.bfloat16)
    given = [pltpu.with_memory_space_constraint(a, pltpu.MemorySpace.HBM) for a in given]
    return pl.pallas_call(
        functools.partial(pack_kernel, expert_count),
        out_shape=(shape, shape),
        in_specs=[pl.BlockSpec(memory_space=pltpu.MemorySpace.HBM)] * 6,
        scratch_shapes=[pltpu.VMEM(a.shape, a.dtype) for a in given] + [pltpu.SemaphoreType.DMA((6,))],
        compiler_params=pltpu.CompilerParams(vmem_limit_bytes=2 << 20),
        cost_estimate=pl.CostEstimate(flops=40_000_000_000, bytes_accessed=100_000_000, transcendentals=0),
        name="pack",
    )(*given)


def chunks(total, size):
    return [(at, min(size, total - at)) for at in range(0, total, size)]


def section_start(j, width, sections):
    if sections == 1:
        return 0
    return pl.multiple_of((lax.axis_index("section") ^ j) * width, LANES)


def field_of(meta, index):
    lane = lax.broadcasted_iota(jnp.int32, meta.shape, 1)
    return jnp.sum(jnp.where(lane == index, meta, 0.0), axis=1, keepdims=True)


def load_rows(groups, sections, width, pieces, held):
    at, metas = 0, []
    for g in range(groups):
        count = pieces[g * sections].shape[0]
        for j in range(sections):
            start = section_start(j, width, sections)
            held[at : at + count, pl.ds(start, width)] = pieces[g * sections + j][:, :width]
        metas.append(pieces[g * sections][:, width:].astype(jnp.float32))
        at += count
    return metas[0] if groups == 1 else jnp.concatenate(metas, axis=0)


def store_rows(groups, sections, width, outs, product):
    for j in range(sections):
        start = section_start(j, width, sections)
        for at, size in chunks(width, 256):
            y = product(start + at, size).astype(jnp.bfloat16)
            row = 0
            for g in range(groups):
                out = outs[g * sections + j]
                out[:, at : at + size] = y[row : row + out.shape[0], :]
                row += out.shape[0]


def hidden_kernel(groups, sections, width, experts, *refs):
    n = groups * sections
    pieces, (gate, up), (hidden, scale), (held,) = refs[:n], refs[n : n + 2], refs[n + 2 : n + 4], refs[n + 4 :]
    meta = load_rows(groups, sections, width, pieces, held)
    me = lax.axis_index("expert")
    scale[...] = field_of(meta, me) + field_of(meta, me + experts)
    for at, size in chunks(hidden.shape[1], 128):
        g = last_last(gate[at : at + size, :], held[...])
        u = last_last(up[at : at + size, :], held[...])
        hidden[:, at : at + size] = (g / (1.0 + jnp.exp(-g)) * u).T.astype(jnp.bfloat16)


def down_kernel(groups, sections, width, hidden, scale, down, *outs):
    store_rows(
        groups, sections, width, outs,
        lambda start, size: last_first(hidden[...], down[:, pl.ds(start, size)]) * scale[...],
    )


def sender_of_rows(rows, tokens, order, me):
    place = lax.broadcasted_iota(jnp.int32, (rows, 1), 0) // tokens
    block = jnp.zeros((rows, 1), jnp.int32) if order is None else jnp.full((rows, 1), me)
    for bit in range((rows // tokens - 1).bit_length()):
        block = block ^ (place >> bit & 1) * (1 << bit if order is None else order[1 << bit])
    return block


def backward_kernel(groups, sections, width, experts, capacity, tokens, order, *refs):
    n = groups * sections
    pieces, (gate_saved, up_saved, gate, up, down) = refs[:n], refs[n : n + 5]
    outs, (held, grad_gate, grad_up) = refs[n + 5 : 2 * n + 5], refs[2 * n + 5 :]
    meta = load_rows(groups, sections, width, pieces, held)
    me = lax.axis_index("expert")
    weight = field_of(meta, me) + field_of(meta, me + experts)
    block = sender_of_rows(held.shape[0], tokens, order, me)
    slot = block * capacity + field_of(meta, me + 2 * experts).astype(jnp.int32)
    slot = jnp.where(weight > 0.0, slot, -1)
    place = lax.broadcasted_iota(jnp.int32, (held.shape[0], gate_saved.shape[0]), 1)
    pick = jnp.where(place == slot, 1.0, 0.0).astype(jnp.bfloat16)
    for at, size in chunks(grad_gate.shape[1], 128):
        part = slice(at, at + size)
        grad = last_last(down[part, :], held[...]).T * weight
        g = last_first(pick, gate_saved[:, part])
        u = last_first(pick, up_saved[:, part])
        q = 1.0 / (1.0 + jnp.exp(-g))
        grad_gate[:, part] = (grad * u * q * (1.0 + g * (1.0 - q))).astype(jnp.bfloat16)
        grad_up[:, part] = (grad * g * q).astype(jnp.bfloat16)
    store_rows(
        groups, sections, width, outs,
        lambda start, size: last_first(grad_gate[...], gate[:, pl.ds(start, size)])
        + last_first(grad_up[...], up[:, pl.ds(start, size)]),
    )


def expert_call(kernel, name, shapes, weights, given, scratch=()):
    rows = given[0].shape[0]
    weights = [pltpu.with_memory_space_constraint(w, VMEM) for w in weights]
    cost = pl.CostEstimate(
        flops=sum(256 * w.size for w in weights), bytes_accessed=sum(2 * w.size for w in weights), transcendentals=0
    )
    return pl.pallas_call(
        kernel,
        out_shape=shapes,
        scratch_shapes=scratch,
        compiler_params=pltpu.CompilerParams(vmem_limit_bytes=24 << 20),
        cost_estimate=cost,
        name=name,
    )(*given, *weights)


def like_pieces(pieces, width):
    return tuple(jax.ShapeDtypeStruct((p.shape[0], width), jnp.bfloat16) for p in pieces)


def rows_of(pieces, sections):
    return sum(p.shape[0] for p in pieces) // sections


def forward_hidden(pieces, sections, width, experts, weights):
    rows, (units, features) = rows_of(pieces, sections), weights[0].shape
    return expert_call(
        functools.partial(hidden_kernel, len(pieces) // sections, sections, width, experts),
        "forward_hidden",
        (jax.ShapeDtypeStruct((rows, units), jnp.bfloat16), jax.ShapeDtypeStruct((rows, 1), jnp.float32)),
        weights, pieces, [pltpu.VMEM((rows, features), jnp.bfloat16)],
    )


def forward_down(pieces, sections, width, hidden, scale, weight):
    return expert_call(
        functools.partial(down_kernel, len(pieces) // sections, sections, width),
        "forward_down", like_pieces(pieces, width), [weight], [hidden, scale],
    )


def experts_backward(pieces, sections, width, experts, capacity, tokens, order, stash, weights):
    rows, (units, features) = rows_of(pieces, sections), weights[0].shape
    return expert_call(
        functools.partial(
            backward_kernel, len(pieces) // sections, sections, width, experts, capacity, tokens, order
        ),
        "experts_backward", like_pieces(pieces, width), weights, [*pieces, *stash],
        [pltpu.VMEM((rows, features), jnp.bfloat16)] + [pltpu.VMEM((rows, units), jnp.bfloat16)] * 2,
    )


def move(value, mask, devices):
    return lax.ppermute(value, AXES, [(i, i ^ mask) for i in range(devices)])


Z = (8, 4, 12)
X, Y, CORE = 2, 16, 1


def after(value, *others):
    return lax.optimization_barrier((value, *others))[0]


def spread_line(message):
    tokens, cols = message.shape
    held = message[None]
    for mask in Z[:2]:
        held = jnp.concatenate([held, move(held, mask, 32)], axis=0)
    return held.reshape(4 * tokens, cols)


def spread_shot(message):
    parts = [move(message, mask, 32) for mask in Z[::-1]][::-1]
    return jnp.concatenate([message, *parts], axis=0)


def spread_plane(held):
    return [held, move(held, Y, 32), move(held, X, 32), move(held, X ^ Y, 32)]


def swap(pieces):
    return [move(p, CORE, 32) for p in pieces[::-1]][::-1]


def add(*parts):
    return sum(p.astype(jnp.float32) for p in parts).astype(jnp.bfloat16)


def collect_plane(own):
    return add(own[0], move(own[3], X ^ Y, 32), move(own[1], Y, 32), move(own[2], X, 32))


def collect_line(total, tokens):
    rows = [total[k * tokens : (k + 1) * tokens] for k in range(4)]
    return add(rows[0], *[move(rows[k + 1], Z[k], 32) for k in (2,0,1)])


def spread_any(message, width):
    held = lax.all_gather(message, "expert", axis=0, tiled=True)
    whole = lax.all_gather(held[:, :width], "section", axis=1, tiled=True)
    return [jnp.concatenate([whole, held[:, width:]], axis=1)]


def collect_any(pieces):
    summed = lax.psum_scatter(pieces[0], "section", scatter_dimension=1, tiled=True)
    return lax.psum_scatter(summed, "expert", scatter_dimension=0, tiled=True)


def shards(
    forward_input, forward_route, forward_weight, output_grad, backward_route, backward_weight,
    gate_stash, up_stash, gate_matrix, up_matrix, down_matrix,
):
    expert_count, section_count = lax.axis_size("expert"), lax.axis_size("section")
    tokens, width = forward_input.shape
    capacity = gate_stash.shape[1] // expert_count
    weights = (gate_matrix[0], up_matrix[0], down_matrix[0])
    stash = (gate_stash[0], up_stash[0])
    message_f, message_b = pack(
        expert_count, forward_input, forward_route, forward_weight, output_grad, backward_route, backward_weight
    )
    if (section_count, expert_count) != (2, 16):
        whole = width * section_count
        pieces_f, pieces_b = spread_any(message_f, width), spread_any(message_b, width)
        hidden, scale = forward_hidden(pieces_f, 1, whole, expert_count, weights[:2])
        done_f = forward_down(pieces_f, 1, whole, hidden, scale, weights[2])
        done_b = experts_backward(pieces_b, 1, whole, expert_count, capacity, tokens, None, stash, weights)
        return collect_any(done_f), collect_any(done_b)
    order = [c ^ x ^ z for c in (0, CORE) for x in (0, X) for z in (0, *Z)]
    line_b, line_f = spread_shot(message_b), spread_line(message_f)
    plane_b = spread_plane(line_b)
    plane_f = spread_plane(line_f)
    pieces_b = plane_b + swap(plane_b)
    done_b = experts_backward(pieces_b, 2, width, expert_count, capacity, tokens, order, stash, weights)
    plane_f = [line_f] + [after(p, done_b[0]) for p in plane_f[1:]]
    pieces_f = plane_f + swap(plane_f)
    hidden, scale = forward_hidden(pieces_f, 2, width, expert_count, weights[:2])
    own_b = [add(a, b) for a, b in zip(done_b[:4], swap(done_b[4:]))]
    done_f = forward_down(pieces_f, 2, width, hidden, scale, weights[2])
    own_f = [add(a, b) for a, b in zip(done_f[:4], swap(done_f[4:]))]
    return collect_line(collect_plane(own_f), tokens), collect_line(collect_plane(own_b), tokens)


def solution(mesh):
    split, rows, stash, matrix = (
        P("expert", "section"), P("expert", None), P("expert", None, "section"), P("expert", "section", None)
    )
    in_specs = (split, rows, rows, split, rows, rows, stash, stash, matrix, matrix, matrix)
    return jax.shard_map(shards, mesh=mesh, in_specs=in_specs, out_specs=(split, split), check_vma=False)
```

```python
import functools

import jax
import jax.numpy as jnp
from jax import lax
from jax.experimental import pallas as pl
from jax.experimental.pallas import tpu as pltpu
from jax.sharding import PartitionSpec as P

LANES = 128
AXES = ("section", "expert")
VMEM = pltpu.MemorySpace.VMEM


def last_last(a, b):
    return lax.dot_general(a, b, (((1,), (1,)), ((), ())), preferred_element_type=jnp.float32)


def last_first(a, b):
    return lax.dot_general(a, b, (((1,), (0,)), ((), ())), preferred_element_type=jnp.float32)


def pack_kernel(expert_count, *refs):
    given, (of, ob), held, arrived = refs[:6], refs[6:8], refs[8:14], refs[14]
    copies = [pltpu.make_async_copy(a, b, arrived.at[i]) for i, (a, b) in enumerate(zip(given, held))]
    for copy in copies:
        copy.start()
    for copy in copies:
        copy.wait()
    xf, rf, wf, xb, rb, wb = held
    tokens, topk = rf.shape
    cols = xf.shape[1]
    lane = lax.broadcasted_iota(jnp.int32, (tokens, LANES), 1)
    row = lax.broadcasted_iota(jnp.int32, (tokens, LANES), 0)
    expert, field = lane % expert_count, lane // expert_count
    for x, r, w, o in ((xf, rf, wf, of), (xb, rb, wb, ob)):
        weight = jnp.zeros((tokens, LANES), jnp.float32)
        named = jnp.zeros((tokens, LANES), jnp.float32)
        for k in range(topk):
            hit = expert == r[:, k : k + 1]
            weight = jnp.where(hit, w[:, k : k + 1], weight)
            named = jnp.where(hit, 1.0, named)
        earlier = jnp.zeros((tokens, LANES), jnp.float32)
        for t in range(tokens - 1):
            earlier = earlier + jnp.where(row > t, named[t : t + 1, :], 0.0)
        high = weight.astype(jnp.bfloat16).astype(jnp.float32)
        low = weight - high
        extra = jnp.where(field == 0, high, jnp.where(field == 1, low, jnp.where(field == 2, earlier, 0.0)))
        o[:, :cols] = x[...]
        o[:, cols:] = extra.astype(jnp.bfloat16)


def pack(expert_count, *given):
    tokens, cols = given[0].shape
    shape = jax.ShapeDtypeStruct((tokens, cols + LANES), jnp.bfloat16)
    given = [pltpu.with_memory_space_constraint(a, pltpu.MemorySpace.HBM) for a in given]
    return pl.pallas_call(
        functools.partial(pack_kernel, expert_count),
        out_shape=(shape, shape),
        in_specs=[pl.BlockSpec(memory_space=pltpu.MemorySpace.HBM)] * 6,
        scratch_shapes=[pltpu.VMEM(a.shape, a.dtype) for a in given] + [pltpu.SemaphoreType.DMA((6,))],
        compiler_params=pltpu.CompilerParams(vmem_limit_bytes=2 << 20),
        cost_estimate=pl.CostEstimate(flops=40_000_000_000, bytes_accessed=100_000_000, transcendentals=0),
        name="pack",
    )(*given)


def chunks(total, size):
    return [(at, min(size, total - at)) for at in range(0, total, size)]


def section_start(j, width, sections):
    if sections == 1:
        return 0
    return pl.multiple_of((lax.axis_index("section") ^ j) * width, LANES)


def field_of(meta, index):
    lane = lax.broadcasted_iota(jnp.int32, meta.shape, 1)
    return jnp.sum(jnp.where(lane == index, meta, 0.0), axis=1, keepdims=True)


def load_rows(groups, sections, width, pieces, held):
    at, metas = 0, []
    for g in range(groups):
        count = pieces[g * sections].shape[0]
        for j in range(sections):
            start = section_start(j, width, sections)
            held[at : at + count, pl.ds(start, width)] = pieces[g * sections + j][:, :width]
        metas.append(pieces[g * sections][:, width:].astype(jnp.float32))
        at += count
    return metas[0] if groups == 1 else jnp.concatenate(metas, axis=0)


def store_rows(groups, sections, width, outs, product):
    for j in range(sections):
        start = section_start(j, width, sections)
        for at, size in chunks(width, 256):
            y = product(start + at, size).astype(jnp.bfloat16)
            row = 0
            for g in range(groups):
                out = outs[g * sections + j]
                out[:, at : at + size] = y[row : row + out.shape[0], :]
                row += out.shape[0]


def hidden_kernel(groups, sections, width, experts, *refs):
    n = groups * sections
    pieces, (gate, up), (hidden, scale), (held,) = refs[:n], refs[n : n + 2], refs[n + 2 : n + 4], refs[n + 4 :]
    meta = load_rows(groups, sections, width, pieces, held)
    me = lax.axis_index("expert")
    scale[...] = field_of(meta, me) + field_of(meta, me + experts)
    for at, size in chunks(hidden.shape[1], 128):
        g = last_last(gate[at : at + size, :], held[...])
        u = last_last(up[at : at + size, :], held[...])
        hidden[:, at : at + size] = (g / (1.0 + jnp.exp(-g)) * u).T.astype(jnp.bfloat16)


def down_kernel(groups, sections, width, hidden, scale, down, *outs):
    store_rows(
        groups, sections, width, outs,
        lambda start, size: last_first(hidden[...], down[:, pl.ds(start, size)]) * scale[...],
    )


def sender_of_rows(rows, tokens, order, me):
    place = lax.broadcasted_iota(jnp.int32, (rows, 1), 0) // tokens
    block = jnp.zeros((rows, 1), jnp.int32) if order is None else jnp.full((rows, 1), me)
    for bit in range((rows // tokens - 1).bit_length()):
        block = block ^ (place >> bit & 1) * (1 << bit if order is None else order[1 << bit])
    return block


def backward_kernel(groups, sections, width, experts, capacity, tokens, order, *refs):
    n = groups * sections
    pieces, (gate_saved, up_saved, gate, up, down) = refs[:n], refs[n : n + 5]
    outs, (held, grad_gate, grad_up) = refs[n + 5 : 2 * n + 5], refs[2 * n + 5 :]
    meta = load_rows(groups, sections, width, pieces, held)
    me = lax.axis_index("expert")
    weight = field_of(meta, me) + field_of(meta, me + experts)
    block = sender_of_rows(held.shape[0], tokens, order, me)
    slot = block * capacity + field_of(meta, me + 2 * experts).astype(jnp.int32)
    slot = jnp.where(weight > 0.0, slot, -1)
    place = lax.broadcasted_iota(jnp.int32, (held.shape[0], gate_saved.shape[0]), 1)
    pick = jnp.where(place == slot, 1.0, 0.0).astype(jnp.bfloat16)
    for at, size in chunks(grad_gate.shape[1], 128):
        part = slice(at, at + size)
        grad = last_last(down[part, :], held[...]).T * weight
        g = last_first(pick, gate_saved[:, part])
        u = last_first(pick, up_saved[:, part])
        q = 1.0 / (1.0 + jnp.exp(-g))
        grad_gate[:, part] = (grad * u * q * (1.0 + g * (1.0 - q))).astype(jnp.bfloat16)
        grad_up[:, part] = (grad * g * q).astype(jnp.bfloat16)
    store_rows(
        groups, sections, width, outs,
        lambda start, size: last_first(grad_gate[...], gate[:, pl.ds(start, size)])
        + last_first(grad_up[...], up[:, pl.ds(start, size)]),
    )


def expert_call(kernel, name, shapes, weights, given, scratch=()):
    rows = given[0].shape[0]
    weights = [pltpu.with_memory_space_constraint(w, VMEM) for w in weights]
    cost = pl.CostEstimate(
        flops=sum(256 * w.size for w in weights), bytes_accessed=sum(2 * w.size for w in weights), transcendentals=0
    )
    return pl.pallas_call(
        kernel,
        out_shape=shapes,
        scratch_shapes=scratch,
        compiler_params=pltpu.CompilerParams(vmem_limit_bytes=8 << 20),
        cost_estimate=cost,
        name=name,
    )(*given, *weights)


def like_pieces(pieces, width):
    return tuple(jax.ShapeDtypeStruct((p.shape[0], width), jnp.bfloat16) for p in pieces)


def rows_of(pieces, sections):
    return sum(p.shape[0] for p in pieces) // sections


def forward_hidden(pieces, sections, width, experts, weights):
    rows, (units, features) = rows_of(pieces, sections), weights[0].shape
    return expert_call(
        functools.partial(hidden_kernel, len(pieces) // sections, sections, width, experts),
        "forward_hidden",
        (jax.ShapeDtypeStruct((rows, units), jnp.bfloat16), jax.ShapeDtypeStruct((rows, 1), jnp.float32)),
        weights, pieces, [pltpu.VMEM((rows, features), jnp.bfloat16)],
    )


def forward_down(pieces, sections, width, hidden, scale, weight):
    return expert_call(
        functools.partial(down_kernel, len(pieces) // sections, sections, width),
        "forward_down", like_pieces(pieces, width), [weight], [hidden, scale],
    )


def experts_backward(pieces, sections, width, experts, capacity, tokens, order, stash, weights):
    rows, (units, features) = rows_of(pieces, sections), weights[0].shape
    return expert_call(
        functools.partial(
            backward_kernel, len(pieces) // sections, sections, width, experts, capacity, tokens, order
        ),
        "experts_backward", like_pieces(pieces, width), weights, [*pieces, *stash],
        [pltpu.VMEM((rows, features), jnp.bfloat16)] + [pltpu.VMEM((rows, units), jnp.bfloat16)] * 2,
    )


def move(value, mask, devices):
    return lax.ppermute(value, AXES, [(i, i ^ mask) for i in range(devices)])


Z = (8, 4, 12)
X, Y, CORE = 2, 16, 1


def after(value, *others):
    return lax.optimization_barrier((value, *others))[0]


def spread_line(message):
    tokens, cols = message.shape
    held = message[None]
    for mask in Z[:2]:
        held = jnp.concatenate([held, move(held, mask, 32)], axis=0)
    return held.reshape(4 * tokens, cols)


def spread_shot(message):
    parts = [move(message, mask, 32) for mask in Z[::-1]][::-1]
    return jnp.concatenate([message, *parts], axis=0)


def spread_plane(held):
    diagonal = move(held, X ^ Y, 32)
    return [held, move(held, Y, 32), move(held, X, 32), diagonal]


def swap(pieces):
    return [move(p, CORE, 32) for p in pieces[::-1]][::-1]


def add(*parts):
    return sum(p.astype(jnp.float32) for p in parts).astype(jnp.bfloat16)


def collect_plane(own):
    return add(own[0], move(own[3], X ^ Y, 32), move(own[1], Y, 32), move(own[2], X, 32))


def collect_line(total, tokens):
    rows = [total[k * tokens : (k + 1) * tokens] for k in range(4)]
    return add(rows[0], *[move(rows[k + 1], Z[k], 32) for k in (2,0,1)])


def spread_any(message, width):
    held = lax.all_gather(message, "expert", axis=0, tiled=True)
    whole = lax.all_gather(held[:, :width], "section", axis=1, tiled=True)
    return [jnp.concatenate([whole, held[:, width:]], axis=1)]


def collect_any(pieces):
    summed = lax.psum_scatter(pieces[0], "section", scatter_dimension=1, tiled=True)
    return lax.psum_scatter(summed, "expert", scatter_dimension=0, tiled=True)


def shards(
    forward_input, forward_route, forward_weight, output_grad, backward_route, backward_weight,
    gate_stash, up_stash, gate_matrix, up_matrix, down_matrix,
):
    expert_count, section_count = lax.axis_size("expert"), lax.axis_size("section")
    tokens, width = forward_input.shape
    capacity = gate_stash.shape[1] // expert_count
    weights = (gate_matrix[0], up_matrix[0], down_matrix[0])
    stash = (gate_stash[0], up_stash[0])
    message_f, message_b = pack(
        expert_count, forward_input, forward_route, forward_weight, output_grad, backward_route, backward_weight
    )
    if (section_count, expert_count) != (2, 16):
        whole = width * section_count
        pieces_f, pieces_b = spread_any(message_f, width), spread_any(message_b, width)
        hidden, scale = forward_hidden(pieces_f, 1, whole, expert_count, weights[:2])
        done_f = forward_down(pieces_f, 1, whole, hidden, scale, weights[2])
        done_b = experts_backward(pieces_b, 1, whole, expert_count, capacity, tokens, None, stash, weights)
        return collect_any(done_f), collect_any(done_b)
    order = [c ^ x ^ z for c in (0, CORE) for x in (0, X) for z in (0, *Z)]
    line_b, line_f = spread_shot(message_b), spread_line(message_f)
    plane_b = spread_plane(line_b)
    plane_f = spread_plane(line_f)
    pieces_b = plane_b + swap(plane_b)
    done_b = experts_backward(pieces_b, 2, width, expert_count, capacity, tokens, order, stash, weights)
    plane_f = [line_f] + [after(p, done_b[0]) for p in plane_f[1:]]
    pieces_f = plane_f + swap(plane_f)
    hidden, scale = forward_hidden(pieces_f, 2, width, expert_count, weights[:2])
    own_b = [add(a, b) for a, b in zip(done_b[:4], swap(done_b[4:]))]
    done_f = forward_down(pieces_f, 2, width, hidden, scale, weights[2])
    own_f = [add(a, b) for a, b in zip(done_f[:4], swap(done_f[4:]))]
    return collect_line(collect_plane(own_f), tokens), collect_line(collect_plane(own_b), tokens)


def solution(mesh):
    split, rows, stash, matrix = (
        P("expert", "section"), P("expert", None), P("expert", None, "section"), P("expert", "section", None)
    )
    in_specs = (split, rows, rows, split, rows, rows, stash, stash, matrix, matrix, matrix)
    return jax.shard_map(shards, mesh=mesh, in_specs=in_specs, out_specs=(split, split), check_vma=False)
```
